128 devices in a mesh: grp: 8 (over x, y_lo), tp: 16 (over z, y_hi, core).
Axes of the slice: x: 4, y: 4 (y_hi: 2, y_lo: 2; y = y_hi * 2 + y_lo), z: 4, core: 2. Of those that a mesh axis runs over, the one named last changes fastest.
Arguments:
- vision_in: bfloat16 [4096, 3200], P(('grp', 'tp')), may hold values from -6 to 6
- vis_gain: float32 [3200], replicated, may hold values from 0.5 to 2
- first_weight: bfloat16 [3200, 12800], P(None, 'tp'), may hold values from -0.109375 to 0.109375
- second_weight: bfloat16 [12800, 3200], P('tp'), may hold values from -0.0546875 to 0.0546875
- layer_scale: float32 [3200], replicated, may hold values from 0.3 to 1.5
- proj_gain: float32 [12800], replicated, may hold values from 0.5 to 2
- proj_weight: bfloat16 [12800, 8192], P(None, 'tp'), may hold values from -0.0546875 to 0.0546875
- text_embed: bfloat16 [9216, 8192], P('grp', 'tp'), may hold values from -6 to 6
- dest_row: int32 [1024], replicated, may hold values from 0 to 9215, as said below
- cotangent: bfloat16 [9216, 8192], P('grp', 'tp'), may hold values from -6 to 6
Outputs:
- seq_embed: bfloat16 [9216, 8192], P('grp', 'tp')
- grad_vision: bfloat16 [4096, 3200], P(('grp', 'tp'))
The draws below stay inside these ranges and needn't reach their ends.
Inputs may be any that keep to these rules, and one draw needn't show every extreme that they name: `dest_row`: all values distinct. Sequence h is rows h * 1152 to (h + 1) * 1152 - 1. The 128 merged rows of index g of grp form four images of 32 rows each; each image fills consecutive token rows of its own sequence, four different sequences for one index of grp, inside positions g * (144) to (g + 1) * 144 - 1 of that sequence. Image j of index g goes to sequence (g + k_j) mod 8 with four distinct shifts k_j common to all g, among them 1 and 4; so at most, and exactly, 32 rows go from one index of grp to one sequence, and every sequence receives four images from four different indices of grp.
All inputs are finite; a program needn't handle non-finite values.
Results may differ from the reference program's by a relative error of at most 0.025.
Values may be sent and summed in bfloat16 or wider, within the bound.
A program may use at most 128 MiB of HBM per device.

```python
import math
import jax
import jax.numpy as jnp
from jax import lax

VD = 3200
VFF = 12800
LD = 8192
SEQ_LEN = 1152
PD = 12800
MROWS_DEV = 128
PATCHES = 4096
MROWS = 1024
TOKENS = 9216


def draw_dest_row(key, part):
    groups = MROWS // MROWS_DEV
    run_len = MROWS_DEV // 4
    region = SEQ_LEN // groups
    half_way = groups // 2
    key_one, key_two = jax.random.split(key, 2)
    shuffled = jax.random.permutation(key_one, groups).astype(jnp.int32)
    flagged = jnp.logical_or(shuffled == 1, shuffled == half_way).astype(jnp.int32)
    ranking = jnp.argsort(flagged * groups + jnp.arange(groups, dtype=jnp.int32), stable=True)
    others = shuffled[ranking][:2]
    shifts = jnp.concatenate([jnp.array([1, half_way], dtype=jnp.int32), others]).astype(jnp.int32)
    sources = jnp.arange(groups, dtype=jnp.int32)
    targets = (sources[:, None] + shifts[None, :]) % groups
    offsets = jax.random.randint(key_two, (groups, 4), 0, region - run_len + 1)
    starts = targets * SEQ_LEN + sources[:, None] * region + offsets
    rows = starts[:, :, None] + jnp.arange(run_len, dtype=jnp.int32)[None, None, :]
    return rows.reshape(-1).astype(jnp.int32)


def level_of(own_key, dims, cuts, low, top_value):
    gain, own = 1.0, jax.random.fold_in(own_key, 6)
    for position, blocks in cuts:
        steps = jnp.exp(jax.random.uniform(jax.random.fold_in(own, position), (blocks,), jnp.float32, low / len(cuts), top_value / len(cuts)))
        gain = gain * jnp.repeat(steps, dims[position] // blocks).reshape([-1 if axis == position else 1 for axis in range(len(dims))])
    return gain


def noise(rng, extent, spread, limit, shards=(), held_as=jnp.bfloat16):
    level = level_of(rng, extent, shards, -0.22, 0.18) if shards else 1.0
    result = jax.random.normal(rng, extent, jnp.float32) * spread * level
    return jnp.minimum(jnp.maximum(result, -limit), limit).astype(held_as)


def setup_inputs(seed: int = 0) -> dict:
    splits = jax.random.split(jax.random.key(seed), 11)
    vision_in = noise(splits[0], (PATCHES, VD), 1.0, 6.0, ((0, 128),))
    vis_gain = jnp.clip(jnp.exp(jax.random.uniform(splits[1], (VD,), jnp.float32, math.log(0.5), math.log(2.0))), 0.5, 2.0)
    first_weight = noise(splits[2], (VD, VFF), VD ** -0.5, 0.109375, ((1, 16),))
    second_weight = noise(splits[3], (VFF, VD), VFF ** -0.5, 0.0546875, ((0, 16),))
    layer_scale = jnp.clip(jnp.exp(jax.random.uniform(splits[4], (VD,), jnp.float32, math.log(0.3), math.log(1.5))), 0.3, 1.5)
    proj_gain = jnp.clip(jnp.exp(jax.random.uniform(splits[5], (PD,), jnp.float32, math.log(0.5), math.log(2.0))), 0.5, 2.0)
    proj_weight = noise(splits[6], (PD, LD), PD ** -0.5, 0.0546875, ((1, 16),))
    text_embed = noise(splits[7], (TOKENS, LD), 1.0, 6.0, ((0, 8), (1, 16)))
    dest_row = draw_dest_row(jax.random.fold_in(splits[10], 71), 0)
    cotangent = noise(splits[9], (TOKENS, LD), 1.0, 6.0, ((0, 8), (1, 16)))
    return dict(vision_in=vision_in, vis_gain=vis_gain, first_weight=first_weight, second_weight=second_weight, layer_scale=layer_scale, proj_gain=proj_gain, proj_weight=proj_weight, text_embed=text_embed, dest_row=dest_row, cotangent=cotangent)


vis_eps = 1e-06
proj_eps = 1e-05

def layer_norm(values, scale_vec, epsilon):
    mean_val = lax.optimization_barrier(jnp.mean(values, -1, keepdims=True))
    centred = values - mean_val
    inv_std = lax.rsqrt(lax.optimization_barrier(jnp.mean(centred * centred, -1, keepdims=True)) + epsilon)
    normed = centred * inv_std
    return (normed * scale_vec, normed, inv_std)

def norm_back(upstream, scale_vec, normed, inv_std):
    scaled = upstream * scale_vec
    return inv_std * (scaled - lax.optimization_barrier(jnp.mean(scaled, -1, keepdims=True)) - normed * lax.optimization_barrier(jnp.mean(scaled * normed, -1, keepdims=True)))

def gelu_slope(values):
    cumul = 0.5 * (1.0 + lax.erf(values * 0.7071067811865476))
    dense = jnp.exp(-0.5 * values * values) * 0.3989422804014327
    return cumul + values * dense

def reference(vision_in, vis_gain, first_weight, second_weight, layer_scale, proj_gain, proj_weight, text_embed, dest_row, cotangent):
    patch_float = vision_in.astype(jnp.float32)
    normed_in, patch_hat, patch_inv = layer_norm(patch_float, vis_gain, vis_eps)
    first_pre = jnp.dot(normed_in.astype(jnp.bfloat16), first_weight, preferred_element_type=jnp.float32)
    hidden = jax.nn.gelu(first_pre, approximate=False).astype(jnp.bfloat16)
    summed = jnp.dot(hidden, second_weight, preferred_element_type=jnp.float32)
    outputs = (patch_float + layer_scale * summed).astype(jnp.bfloat16)
    merged = outputs.reshape(MROWS, PD)
    merged_norm, merged_hat, merged_inv = layer_norm(merged.astype(jnp.float32), proj_gain, proj_eps)
    proj_pre = jnp.dot(merged_norm.astype(jnp.bfloat16), proj_weight, preferred_element_type=jnp.float32)
    projected = jax.nn.gelu(proj_pre, approximate=False).astype(jnp.bfloat16)
    seq_embed = text_embed.at[dest_row].set(projected)
    grad_proj = cotangent[dest_row]
    proj_delta = (grad_proj.astype(jnp.float32) * gelu_slope(proj_pre)).astype(jnp.bfloat16)
    back_sum = jnp.dot(proj_delta, proj_weight.T, preferred_element_type=jnp.float32)
    merged_grad = norm_back(back_sum, proj_gain, merged_hat, merged_inv).astype(jnp.bfloat16)
    grad_out = merged_grad.reshape(PATCHES, VD)
    scaled_grad = (grad_out.astype(jnp.float32) * layer_scale).astype(jnp.bfloat16)
    hidden_grad = jnp.dot(scaled_grad, second_weight.T, preferred_element_type=jnp.float32)
    first_delta = (hidden_grad * gelu_slope(first_pre)).astype(jnp.bfloat16)
    normed_grad = jnp.dot(first_delta, first_weight.T, preferred_element_type=jnp.float32)
    grad_vision = (grad_out.astype(jnp.float32) + norm_back(normed_grad, vis_gain, patch_hat, patch_inv)).astype(jnp.bfloat16)
    return (seq_embed, grad_vision)
```

```python
import functools

import jax
import jax.numpy as jnp
from jax import lax
from jax.experimental import pallas as pl
from jax.experimental.pallas import tpu as pltpu
from jax.sharding import Mesh
from jax.sharding import PartitionSpec as P

AXES = ("x", "ylo", "z", "yhi", "core")
GRP = ("x", "ylo")
TP = ("z", "yhi", "core")
MESH = pl.DeviceIdType.MESH
VIS_EPS = 1e-06
PROJ_EPS = 1e-05
F32 = jnp.float32
BF16 = jnp.bfloat16

PLACES = [(0, 0), (1, 0), (-1, 0), (0, 1), (2, 0), (1, 1), (-1, 1), (2, 1)]
PAIR = {place: n for n, place in enumerate(PLACES)}
PAIRS = 8
UNITS = 16
NEAR = (0, 5)
FAR = (5, 8)
QUARTERS = (0, 3, 1, 2)
AG_MSGS = 29
RS_MSGS = 32
PHASE_MSGS = AG_MSGS + RS_MSGS


def erf_half(u):
    return 0.5 * (1.0 + lax.erf(u * 0.7071067811865476))


def gelu(u):
    return u * erf_half(u)


def gelu_slope(u):
    return erf_half(u) + u * (jnp.exp(-0.5 * u * u) * 0.3989422804014327)


def dot(a, b):
    return jnp.dot(a, b, preferred_element_type=F32)


def dot_t(a, b):
    return lax.dot_general(a, b, (((1,), (1,)), ((), ())), preferred_element_type=F32)


def iota(shape, dim):
    return lax.broadcasted_iota(jnp.int32, shape, dim)


def one_hot(cond):
    return jnp.where(cond, 1.0, 0.0).astype(BF16)


def line(ref, start, count):
    return jnp.concatenate([ref[pl.ds(start + n, 1), :] for n in range(count)], axis=1)


def turned(col):
    n = col.shape[0]
    return jnp.sum(jnp.where(iota((n, n), 0) == iota((n, n), 1), col, 0.0), 0, keepdims=True)


def kernel(
    x_ref, vgain_ref, ls_ref, pgain_ref, dest_ref,
    w1_hbm, w2_hbm, wp_hbm, text_hbm, cot_hbm,
    seq_hbm, grad_ref,
    w1, w2, wp, cot, seq,
    g1, g2, g3, part, rcore, rya, rye, rzb, rzc, rzd,
    pre1, hid, pre2, hid2,
    out_slots, arrived, picked, returned,
    xhat, xinv, own, mhat, minv, vgain, ls, pgain,
    scol, srow, tcol, trow,
    ssem, rsem, esend, erecv, lsem,
):
    x = lax.axis_index("x")
    ylo = lax.axis_index("ylo")
    z = lax.axis_index("z")
    yhi = lax.axis_index("yhi")
    core = lax.axis_index("core")
    grp = 2 * x + ylo
    unit_rows, width = x_ref.shape
    half = unit_rows // 2
    merged_own = unit_rows // 4
    merged_all = UNITS * merged_own
    slots = 8 * 32
    seq_len = cot.shape[0]
    to = {
        "y": {"ylo": 1 - ylo, "yhi": 1 - yhi},
        "z+": {"z": lax.rem(z + 1, 4)},
        "z-": {"z": lax.rem(z + 3, 4)},
        "c": {"core": 1 - core},
    }

    def peer(k):
        g = lax.rem(grp + k, 8)
        return g, {"x": g // 2, "ylo": lax.rem(g, 2)}

    barrier = pltpu.get_barrier_semaphore()
    for d in to.values():
        pl.semaphore_signal(barrier, inc=1, device_id=d, device_id_type=MESH)
    for k in range(1, 8):
        pl.semaphore_signal(barrier, inc=1, device_id=peer(k)[1], device_id_type=MESH)

    loads = []
    for n, (src, dst) in enumerate(((cot_hbm, cot), (w1_hbm, w1), (w2_hbm, w2), (wp_hbm, wp), (text_hbm, seq))):
        copy = pltpu.make_async_copy(src, dst, lsem.at[n])
        copy.start()
        loads.append(copy)
    cot_load, w1_load, w2_load, wp_load, text_load = loads

    sent = []

    def remote(src, dst, where, n):
        copy = pltpu.make_async_remote_copy(
            src_ref=src, dst_ref=dst, send_sem=ssem.at[n], recv_sem=rsem.at[n],
            device_id=to[where], device_id_type=MESH,
        )
        sent.append(copy)
        return copy

    def free_part():
        for copy in sent:
            copy.wait_send()
        sent.clear()

    def halves(h):
        return pl.ds(h * half, half)

    def quarter(q):
        return pl.ds(q * merged_own, merged_own)

    def gather(phase, buf, early, middle, late):
        count = iter(range(phase * PHASE_MSGS, phase * PHASE_MSGS + AG_MSGS))

        def msg(src, dst, where, rows=None):
            s, d = buf.at[PAIR[src]], buf.at[PAIR[dst]]
            if rows is not None:
                s, d = s.at[rows], d.at[rows]
            return remote(s, d, where, next(count))

        def cross(first, last):
            return remote(buf.at[first:last], buf.at[PAIRS + first : PAIRS + last], "c", next(count))

        own_zp = [msg((0, 0), (-1, 0), "z+", quarter(q)) for q in range(4)]
        own_zm = [msg((0, 0), (1, 0), "z-", quarter(q)) for q in range(4)]
        own_y = [msg((0, 0), (0, 1), "y", halves(h)) for h in range(2)]
        two = {q: msg((-1, 0), (2, 0), "z+", quarter(q)) for q in (0, 1)}
        two |= {q: msg((1, 0), (2, 0), "z-", quarter(q)) for q in (3, 2)}
        y_zp = [msg((0, 1), (-1, 1), "z+", halves(h)) for h in range(2)]
        y_zm = [msg((0, 1), (1, 1), "z-", halves(h)) for h in range(2)]
        two_y = [msg((2, 0), (2, 1), "y", quarter(q)) for q in range(4)]
        c_own, c_side, c_y, c_two, c_far, c_last = (
            cross(*r) for r in ((0, 1), (1, 3), (3, 4), (4, 5), (5, 7), (7, 8))
        )
        for copy in (
            own_zp[0], own_zm[3], own_y[0], own_zp[1], own_zm[2], own_y[1], own_zp[2], own_zm[1], c_own,
        ):
            copy.start()
        early()
        for p, m in ((0, 3), (1, 2)):
            own_zp[p].wait_recv()
            two[p].start()
            own_zm[m].wait_recv()
            two[m].start()
        own_zp[3].start()
        own_zm[0].start()
        own_y[0].wait_recv()
        y_zp[0].start()
        y_zm[0].start()
        for q in (0, 3):
            two[q].wait_recv()
            two_y[q].start()
        own_y[1].wait_recv()
        y_zp[1].start()
        y_zm[1].start()
        c_y.start()
        for q in (1, 2):
            two[q].wait_recv()
            two_y[q].start()
        c_two.start()
        for copy in (own_zp[2], own_zp[3], own_zm[1], own_zm[0]):
            copy.wait_recv()
        c_side.start()
        for copy in (c_own, c_y, c_two, c_side):
            copy.wait_recv()
        middle()
        for copy in (*y_zp, *y_zm):
            copy.wait_recv()
        c_far.start()
        for copy in two_y:
            copy.wait_recv()
        c_last.start()
        c_far.wait_recv()
        c_last.wait_recv()
        late()

    class Scatter:
        def __init__(self, phase):
            count = iter(range(phase * PHASE_MSGS + AG_MSGS, (phase + 1) * PHASE_MSGS))
            self.phase = phase

            def msg(place, rows, dst, where):
                return remote(part.at[PAIR[place], rows], dst.at[rows], where, next(count))

            def cross(first, last, rows):
                return remote(
                    part.at[PAIRS + first : PAIRS + last, rows], rcore.at[phase, first:last, rows], "c", next(count)
                )

            if phase == 1:
                self.cross = [cross(0, PAIRS, quarter(q)) for q in range(4)]
            else:
                everything = pl.ds(0, unit_rows)
                self.cross = {g: cross(*g, everything) for g in (FAR, NEAR)}
            self.a = [msg((2, 1), quarter(q), rya.at[phase], "y") for q in range(4)]
            self.b = [
                (msg((1, 1), quarter(q), rzb.at[phase, 0], "z+"), msg((-1, 1), quarter(q), rzb.at[phase, 1], "z-"))
                for q in range(4)
            ]
            self.c = [msg((2, 0), quarter(q), rzc.at[phase], "z+" if q < 2 else "z-") for q in range(4)]
            self.dp = [msg((1, 0), quarter(q), rzd.at[phase, 0], "z+") for q in range(4)]
            self.dm = [msg((-1, 0), quarter(q), rzd.at[phase, 1], "z-") for q in range(4)]
            self.e = [msg((0, 1), halves(h), rye.at[phase], "y") for h in range(2)]

        def join(self, first, last, rows):
            for n in range(first, last):
                v = part[n, rows, :].astype(F32) + rcore[self.phase, n, rows, :].astype(F32)
                part[n, rows, :] = v.astype(BF16)

        def add(self, place, rows, *refs):
            n = PAIR[place]
            v = part[n, rows, :].astype(F32)
            for ref in refs:
                v = v + ref[rows, :].astype(F32)
            part[n, rows, :] = v.astype(BF16)

        def leave(self, q):
            self.a[q].start()
            for copy in self.b[q]:
                copy.start()

        def relay(self, idle):
            p = self.phase

            def pass_two(q):
                self.a[q].wait_recv()
                self.add((2, 0), quarter(q), rya.at[p])
                self.c[q].start()

            def pass_y(h):
                for q in (2 * h, 2 * h + 1):
                    for copy in self.b[q]:
                        copy.wait_recv()
                self.add((0, 1), halves(h), rzb.at[p, 0], rzb.at[p, 1])
                self.e[h].start()

            pass_two(0)
            pass_two(3)
            pass_y(0)
            pass_two(1)
            pass_two(2)
            for q in (2, 3):
                self.dp[q].start()
            for q in (1, 0):
                self.dm[q].start()
            pass_y(1)
            for q in QUARTERS:
                self.c[q].wait_recv()
                side, out = ((1, 0), self.dp) if q < 2 else ((-1, 0), self.dm)
                self.add(side, quarter(q), rzc.at[p])
                out[q].start()
            idle()
            for copy in (*self.e, *self.dp, *self.dm):
                copy.wait_recv()
            return (
                part[0].astype(F32) + rzd[p, 0].astype(F32) + rzd[p, 1].astype(F32) + rye[p].astype(F32)
            )

    def units(buf, group):
        a, b = group
        m = 2 * (b - a) * unit_rows
        return jnp.concatenate([buf[a:b], buf[PAIRS + a : PAIRS + b]], axis=0).reshape(m, width)

    def hidden_rows(group):
        return pl.ds(2 * group[0] * unit_rows, 2 * (group[1] - group[0]) * unit_rows)

    def put_parts(group, v):
        a, b = group
        v = v.astype(BF16).reshape(2, b - a, unit_rows, width)
        part[a:b] = v[0]
        part[PAIRS + a : PAIRS + b] = v[1]

    def up(group):
        def go():
            r = hidden_rows(group)
            pre1[r, :] = dot_t(units(g1, group), w1[...])

            def act(i, _):
                s = pl.ds(pl.multiple_of(r.start + i * 32, 32), 32)
                hid[s, :] = gelu(pre1[s, :]).astype(BF16)
                return 0

            lax.fori_loop(0, r.size // 32, act, 0)

        return go

    def down(group):
        put_parts(group, dot(hid[hidden_rows(group), :], w2[...]))

    def up_back(group):
        def go():
            r = hidden_rows(group)
            hid[r, :] = (dot_t(units(g3, group), w2[...]) * pre1[r, :]).astype(BF16)

        return go

    def down_back(group):
        put_parts(group, dot(hid[hidden_rows(group), :], w1[...]))

    def scatter_mlp(phase, compute, idle):
        s = Scatter(phase)
        everything = pl.ds(0, unit_rows)
        compute(FAR)
        s.cross[FAR].start()
        s.cross[FAR].wait_recv()
        s.join(*FAR, everything)
        for q in QUARTERS:
            s.leave(q)
        compute(NEAR)
        s.cross[NEAR].start()
        s.cross[NEAR].wait_recv()
        s.join(*NEAR, everything)
        return s.relay(idle)

    near_row = iota((unit_rows, unit_rows), 0)
    far_row = iota((unit_rows, unit_rows), 1)

    def spread(a, b):
        return one_hot(far_row == lax.rem(near_row, a) * b + near_row // a)

    blocks = width // 128
    vgain[...] = line(vgain_ref, 0, blocks)
    v = dot(spread(merged_own, 4), x_ref[...])
    cen = v - jnp.mean(v, -1, keepdims=True)
    inv = lax.rsqrt(jnp.mean(cen * cen, -1, keepdims=True) + VIS_EPS)
    hat = cen * inv
    xhat[...] = hat
    xinv[...] = inv
    g1[0] = (hat * vgain[...]).astype(BF16)
    own[...] = v

    row = iota((1, dest_ref.size), 1)
    dest = line(dest_ref, 0, dest_ref.shape[0])
    dest_seq = jnp.zeros_like(dest)
    for n in range(1, 8):
        dest_seq += jnp.where(dest >= n * seq_len, 1, 0)
    inside = row & 31
    row_grp = row >> 7
    row_z = (row >> 5) & 3
    row_y = (row >> 4) & 1
    row_core = (row >> 3) & 1
    key = jnp.where(
        dest_seq == grp, ((row_grp & 6) | ((row_grp & 1) ^ row_y ^ yhi)) * 32 + inside, -1
    )
    token = (dest - dest_seq * seq_len + 1).astype(F32)
    tok = jnp.sum(jnp.where(key == iota((slots, row.shape[1]), 0), token, 0.0), -1, keepdims=True) - 1.0
    tcol[...] = tok.astype(jnp.int32)
    trow[...] = turned(tok).astype(jnp.int32)
    step_z = (row_z - z) & 3
    step_y = row_y ^ yhi
    pair = jnp.where(
        step_y == 0,
        jnp.where(step_z == 0, 0, jnp.where(step_z == 1, 1, jnp.where(step_z == 3, 2, 4))),
        jnp.where(step_z == 0, 3, jnp.where(step_z == 1, 5, jnp.where(step_z == 3, 6, 7))),
    )
    mine = ((row_grp >> 1) == x) & (((row_grp & 1) ^ row_y) == (ylo ^ yhi))
    key = jnp.where(mine, ((row_core ^ core) * PAIRS + pair) * merged_own + (row & 7), -1)
    slot = (dest_seq * 32 + inside).astype(F32)
    slot = jnp.sum(jnp.where(key == iota((merged_all, row.shape[1]), 0), slot, 0.0), -1, keepdims=True)
    scol[...] = slot.astype(jnp.int32)
    srow[...] = turned(slot).astype(jnp.int32)
    pl.semaphore_wait(barrier, 11)

    def exchange(src, dst, n):
        copies = []
        for k in range(1, 8):
            g, where = peer(k)
            copies.append(pltpu.make_async_remote_copy(
                src_ref=src.at[g], dst_ref=dst.at[grp],
                send_sem=esend.at[n, k - 1], recv_sem=erecv.at[n, k - 1],
                device_id=where, device_id_type=MESH,
            ))
        copies.append(pltpu.make_async_copy(src.at[grp], dst.at[grp], lsem.at[5 + n]))
        for copy in copies:
            copy.start()
        return copies

    def exchange_wait(copies):
        for copy in copies:
            copy.wait()

    holder = {}

    def pick():
        cot_load.wait()
        v = dot(one_hot(iota((slots, seq_len), 1) == tcol[...]), cot[...])
        picked[...] = v.astype(BF16).reshape(picked.shape)
        holder["cot"] = exchange(picked, returned, 0)

    def up_near():
        w1_load.wait()
        up(NEAR)()
        ls[...] = line(ls_ref, 0, blocks)
        for q in range(4):
            pgain[quarter(q), :] = jnp.broadcast_to(line(pgain_ref, q * blocks, blocks), (merged_own, width))

    def slopes():
        def act(i, _):
            r = pl.ds(pl.multiple_of(i * 32, 32), 32)
            pre1[r, :] = gelu_slope(pre1[r, :])
            return 0

        lax.fori_loop(0, UNITS, act, 0)

    gather(0, g1, pick, up_near, up(FAR))
    w2_load.wait()
    total = scatter_mlp(0, down, slopes)

    def over_merged(v):
        s = jnp.sum(v, -1, keepdims=True).reshape(4, merged_own, 1).sum(axis=0) * (1.0 / (4 * width))
        return jnp.concatenate([s] * 4, axis=0)

    y = (own[...] + ls[...] * total).astype(BF16).astype(F32)
    cen = y - over_merged(y)
    inv = lax.rsqrt(over_merged(cen * cen) + PROJ_EPS)
    hat = cen * inv
    mhat[...] = hat
    minv[...] = inv
    g2[0] = (hat * pgain[...]).astype(BF16)

    def ready():
        wp_load.wait()
        exchange_wait(holder["cot"])

    def project():
        free_part()
        for q in range(4):
            lhs = g2[:, quarter(q), :].reshape(merged_all, width)
            v = dot(lhs, wp[pl.ds(q * width, width), :])
            if q == 0:
                pre2[...] = v
            else:
                pre2[...] += v
        back = dot(one_hot(iota((merged_all, slots), 1) == scol[...]), returned[...].reshape(slots, -1))
        hid2[...] = (back * gelu_slope(pre2[...])).astype(BF16)

    def project_back(q):
        v = dot_t(hid2[...], wp[pl.ds(q * width, width), :])
        part[:, quarter(q), :] = v.astype(BF16).reshape(UNITS, merged_own, width)

    def send_projected():
        v = dot(one_hot(iota((slots, merged_all), 0) == srow[...]), gelu(pre2[...]).astype(BF16))
        out_slots[...] = v.astype(BF16).reshape(out_slots.shape)
        holder["proj"] = exchange(out_slots, arrived, 1)

    gather(1, g2, lambda: None, ready, project)
    s = Scatter(1)

    def far_ready(q):
        s.cross[q].wait_recv()
        s.join(*FAR, quarter(q))
        s.leave(q)

    for n, q in enumerate(QUARTERS):
        project_back(q)
        s.cross[q].start()
        if n:
            far_ready(QUARTERS[n - 1])
    far_ready(QUARTERS[3])
    s.join(*NEAR, pl.ds(0, unit_rows))
    total = s.relay(send_projected)
    hat = mhat[...]
    v = total * pgain[...]
    dm = minv[...] * (v - over_merged(v) - hat * over_merged(v * hat))
    dy = dm.astype(BF16).astype(F32)
    own[...] = dy
    g3[0] = (dy * ls[...]).astype(BF16)

    def fill():
        text_load.wait()
        exchange_wait(holder["proj"])
        block = 128
        flat = arrived[...].reshape(slots, -1)

        def step(i, _):
            r0 = pl.multiple_of(i * block, block)
            r = pl.ds(r0, block)
            hot = jnp.where(iota((block, slots), 0) + r0 == trow[...], 1.0, 0.0)
            v = dot(hot.astype(BF16), flat)
            filled = jnp.sum(hot, -1, keepdims=True) > 0.5
            seq[r, :] = jnp.where(filled, v, seq[r, :].astype(F32)).astype(BF16)
            return 0

        lax.fori_loop(0, seq_len // block, step, 0)
        holder["seq"] = pltpu.make_async_copy(seq, seq_hbm, lsem.at[7])
        holder["seq"].start()

    gather(2, g3, lambda: None, up_back(NEAR), up_back(FAR))
    free_part()
    total = scatter_mlp(2, down_back, fill)
    hat = xhat[...]
    v = total * vgain[...]
    g = own[...] + xinv[...] * (
        v - jnp.mean(v, -1, keepdims=True) - hat * jnp.mean(v * hat, -1, keepdims=True)
    )
    grad_ref[...] = dot(spread(4, merged_own), g.astype(BF16)).astype(BF16)
    free_part()
    holder["seq"].wait()


def junction(x, vgain, ls, pgain, dest, w1, w2, wp, text, cot):
    unit_rows, width = x.shape
    hidden = w1.shape[0]
    cols = wp.shape[1]
    all_rows = UNITS * unit_rows
    merged_all = all_rows // 4
    vmem = pl.BlockSpec(memory_space=pltpu.VMEM)
    hbm = pl.BlockSpec(memory_space=pl.ANY)
    V = pltpu.VMEM
    unit = (unit_rows, width)
    scratch = [
        V(w1.shape, BF16), V(w2.shape, BF16), V(wp.shape, BF16), V(cot.shape, BF16), V(text.shape, BF16),
        *[V((UNITS, *unit), BF16)] * 4,
        V((3, PAIRS, *unit), BF16),
        V((3, *unit), BF16), V((3, *unit), BF16), V((3, 2, *unit), BF16), V((3, *unit), BF16), V((3, 2, *unit), BF16),
        V((all_rows, hidden), F32), V((all_rows, hidden), BF16), V((merged_all, cols), F32), V((merged_all, cols), BF16),
        *[V((8, 32, cols), BF16)] * 4,
        V(unit, F32), V((unit_rows, 1), F32), V(unit, F32), V(unit, F32), V((unit_rows, 1), F32),
        V((1, width), F32), V((1, width), F32), V(unit, F32),
        V((merged_all, 1), jnp.int32), V((1, merged_all), jnp.int32), V((256, 1), jnp.int32), V((1, 256), jnp.int32),
        pltpu.SemaphoreType.DMA((3 * PHASE_MSGS,)), pltpu.SemaphoreType.DMA((3 * PHASE_MSGS,)),
        pltpu.SemaphoreType.DMA((2, 7)), pltpu.SemaphoreType.DMA((2, 7)),
        pltpu.SemaphoreType.DMA((8,)),
    ]
    return pl.pallas_call(
        kernel,
        out_shape=(jax.ShapeDtypeStruct(text.shape, BF16), jax.ShapeDtypeStruct(x.shape, BF16)),
        in_specs=[vmem] * 5 + [hbm] * 5,
        out_specs=(hbm, vmem),
        scratch_shapes=scratch,
        name="junction",
        compiler_params=pltpu.CompilerParams(
            collective_id=0, has_side_effects=True, vmem_limit_bytes=67_000_000
        ),
    )(x, vgain, ls, pgain, dest, w1, w2, wp, text, cot)


def per_device(
    vision_in, vis_gain, first_weight, second_weight, layer_scale,
    proj_gain, proj_weight, text_embed, dest_row, cotangent,
):
    return junction(
        vision_in, vis_gain.reshape(-1, 128), layer_scale.reshape(-1, 128), proj_gain.reshape(-1, 128),
        dest_row.reshape(-1, 128), first_weight.T, second_weight, proj_weight, text_embed, cotangent,
    )


def solution(mesh):
    torus = Mesh(mesh.devices.reshape(4, 2, 4, 2, 2), AXES)
    in_specs = (
        P((*GRP, *TP), None), P(), P(None, TP), P(TP, None), P(), P(), P(None, TP),
        P(GRP, TP), P(), P(GRP, TP),
    )
    out_specs = (P(GRP, TP), P((*GRP, *TP), None))
    return jax.shard_map(per_device, mesh=torus, in_specs=in_specs, out_specs=out_specs, check_vma=False)
```

```python
import functools

import jax
import jax.numpy as jnp
from jax import lax
from jax.experimental import pallas as pl
from jax.experimental.pallas import tpu as pltpu
from jax.sharding import Mesh
from jax.sharding import PartitionSpec as P

AXES = ("x", "ylo", "z", "yhi", "core")
GRP = ("x", "ylo")
TP = ("z", "yhi", "core")
MESH = pl.DeviceIdType.MESH
VIS_EPS = 1e-06
PROJ_EPS = 1e-05
F32 = jnp.float32
BF16 = jnp.bfloat16

PLACES = [(0, 0), (1, 0), (-1, 0), (0, 1), (2, 0), (1, 1), (-1, 1), (2, 1)]
PAIR = {place: n for n, place in enumerate(PLACES)}
PAIRS = 8
UNITS = 16
NEAR = (0, 5)
FAR = (5, 8)
QUARTERS = (0, 3, 1, 2)
AG_MSGS = 30
RS_MSGS = 32
PHASE_MSGS = AG_MSGS + RS_MSGS


def erf_half(u):
    return 0.5 * (1.0 + lax.erf(u * 0.7071067811865476))


def gelu(u):
    return u * erf_half(u)


def gelu_slope(u):
    return erf_half(u) + u * (jnp.exp(-0.5 * u * u) * 0.3989422804014327)


def dot(a, b):
    return jnp.dot(a, b, preferred_element_type=F32)


def dot_t(a, b):
    return lax.dot_general(a, b, (((1,), (1,)), ((), ())), preferred_element_type=F32)


def iota(shape, dim):
    return lax.broadcasted_iota(jnp.int32, shape, dim)


def one_hot(cond):
    return jnp.where(cond, 1.0, 0.0).astype(BF16)


def line(ref, start, count):
    return jnp.concatenate([ref[pl.ds(start + n, 1), :] for n in range(count)], axis=1)


def turned(col):
    n = col.shape[0]
    return jnp.sum(jnp.where(iota((n, n), 0) == iota((n, n), 1), col, 0.0), 0, keepdims=True)


def kernel(
    x_ref, vgain_ref, ls_ref, pgain_ref, dest_ref,
    w1_hbm, w2_hbm, wp_hbm, text_hbm, cot_hbm,
    seq_hbm, grad_ref,
    w1, w2, wp, cot, seq,
    g1, g2, g3, part, rcore, rya, rye, rzb, rzc, rzd,
    pre1, hid, pre2, hid2, back,
    out_slots, arrived, picked, returned,
    xhat, xinv, own, mhat, minv, vgain, ls, pgain,
    scol, srow, tcol, trow,
    ssem, rsem, esend, erecv, lsem,
):
    x = lax.axis_index("x")
    ylo = lax.axis_index("ylo")
    z = lax.axis_index("z")
    yhi = lax.axis_index("yhi")
    core = lax.axis_index("core")
    grp = 2 * x + ylo
    unit_rows, width = x_ref.shape
    half = unit_rows // 2
    merged_own = unit_rows // 4
    merged_all = UNITS * merged_own
    slots = 8 * 32
    seq_len = cot.shape[0]
    to = {
        "y": {"ylo": 1 - ylo, "yhi": 1 - yhi},
        "z+": {"z": lax.rem(z + 1, 4)},
        "z-": {"z": lax.rem(z + 3, 4)},
        "c": {"core": 1 - core},
    }

    def peer(k):
        g = lax.rem(grp + k, 8)
        return g, {"x": g // 2, "ylo": lax.rem(g, 2)}

    barrier = pltpu.get_barrier_semaphore()
    for d in to.values():
        pl.semaphore_signal(barrier, inc=1, device_id=d, device_id_type=MESH)
    for k in range(1, 8):
        pl.semaphore_signal(barrier, inc=1, device_id=peer(k)[1], device_id_type=MESH)

    loads = []
    for n, (src, dst) in enumerate(((cot_hbm, cot), (w1_hbm, w1), (w2_hbm, w2), (wp_hbm, wp), (text_hbm, seq))):
        copy = pltpu.make_async_copy(src, dst, lsem.at[n])
        copy.start()
        loads.append(copy)
    cot_load, w1_load, w2_load, wp_load, text_load = loads

    sent = []

    def remote(src, dst, where, n):
        copy = pltpu.make_async_remote_copy(
            src_ref=src, dst_ref=dst, send_sem=ssem.at[n], recv_sem=rsem.at[n],
            device_id=to[where], device_id_type=MESH,
        )
        sent.append(copy)
        return copy

    def free_part():
        for copy in sent:
            copy.wait_send()
        sent.clear()

    def halves(h):
        return pl.ds(h * half, half)

    def quarter(q):
        return pl.ds(q * merged_own, merged_own)

    def gather(phase, buf, middle, late):
        count = iter(range(phase * PHASE_MSGS, phase * PHASE_MSGS + AG_MSGS))

        def msg(src, dst, where, rows=None):
            s, d = buf.at[PAIR[src]], buf.at[PAIR[dst]]
            if rows is not None:
                s, d = s.at[rows], d.at[rows]
            return remote(s, d, where, next(count))

        def cross(first, last, rows=pl.ds(0, unit_rows)):
            return remote(
                buf.at[first:last, rows], buf.at[PAIRS + first : PAIRS + last, rows], "c", next(count)
            )

        own_zp = [msg((0, 0), (-1, 0), "z+", quarter(q)) for q in range(4)]
        own_zm = [msg((0, 0), (1, 0), "z-", quarter(q)) for q in range(4)]
        own_y = [msg((0, 0), (0, 1), "y", halves(h)) for h in range(2)]
        two = {q: msg((-1, 0), (2, 0), "z+", quarter(q)) for q in (0, 1)}
        two |= {q: msg((1, 0), (2, 0), "z-", quarter(q)) for q in (3, 2)}
        y_zp = [msg((0, 1), (-1, 1), "z+", halves(h)) for h in range(2)]
        y_zm = [msg((0, 1), (1, 1), "z-", halves(h)) for h in range(2)]
        two_y = [msg((2, 0), (2, 1), "y", quarter(q)) for q in range(4)]
        c_own, c_side, c_y, c_two = (cross(*r) for r in ((0, 1), (1, 3), (3, 4), (4, 5)))
        c_far = [cross(5, 7, halves(h)) for h in range(2)]
        c_last = [cross(7, 8, halves(h)) for h in range(2)]
        for copy in (
            own_zp[0], own_zm[3], own_y[0], own_zp[1], own_zm[2], own_y[1], own_zp[2], own_zm[1], c_own,
        ):
            copy.start()
        for p, m in ((0, 3), (1, 2)):
            own_zp[p].wait_recv()
            two[p].start()
            own_zm[m].wait_recv()
            two[m].start()
        own_zp[3].start()
        own_zm[0].start()
        own_y[0].wait_recv()
        y_zp[0].start()
        y_zm[0].start()
        two[0].wait_recv()
        two_y[0].start()
        own_y[1].wait_recv()
        y_zp[1].start()
        y_zm[1].start()
        c_y.start()
        for q in (1, 3, 2):
            two[q].wait_recv()
            two_y[q].start()
        c_two.start()
        for copy in (own_zp[2], own_zp[3], own_zm[1], own_zm[0]):
            copy.wait_recv()
        c_side.start()
        for copy in (c_own, c_y, c_two, c_side):
            copy.wait_recv()
        for h in range(2):
            middle(h)
            y_zp[h].wait_recv()
            y_zm[h].wait_recv()
            c_far[h].start()
            for q in (2 * h, 2 * h + 1):
                two_y[q].wait_recv()
            c_last[h].start()
        for copy in (*c_far, *c_last):
            copy.wait_recv()
        late()

    class Scatter:
        def __init__(self, phase):
            count = iter(range(phase * PHASE_MSGS + AG_MSGS, (phase + 1) * PHASE_MSGS))
            self.phase = phase

            def msg(place, rows, dst, where):
                return remote(part.at[PAIR[place], rows], dst.at[rows], where, next(count))

            def cross(first, last, rows):
                return remote(
                    part.at[PAIRS + first : PAIRS + last, rows], rcore.at[phase, first:last, rows], "c", next(count)
                )

            if phase == 1:
                self.cross = [cross(0, PAIRS, quarter(q)) for q in range(4)]
            else:
                everything = pl.ds(0, unit_rows)
                self.cross = {g: cross(*g, everything) for g in ((5, 7), (7, 8), (4, 5), (1, 4), (0, 1))}
            self.a = [msg((2, 1), quarter(q), rya.at[phase], "y") for q in range(4)]
            self.b = [
                (msg((1, 1), quarter(q), rzb.at[phase, 0], "z+"), msg((-1, 1), quarter(q), rzb.at[phase, 1], "z-"))
                for q in range(4)
            ]
            self.c = [msg((2, 0), quarter(q), rzc.at[phase], "z+" if q < 2 else "z-") for q in range(4)]
            self.dp = [msg((1, 0), quarter(q), rzd.at[phase, 0], "z+") for q in range(4)]
            self.dm = [msg((-1, 0), quarter(q), rzd.at[phase, 1], "z-") for q in range(4)]
            self.e = [msg((0, 1), halves(h), rye.at[phase], "y") for h in range(2)]

        def join(self, first, last, rows):
            for n in range(first, last):
                v = part[n, rows, :].astype(F32) + rcore[self.phase, n, rows, :].astype(F32)
                part[n, rows, :] = v.astype(BF16)

        def add(self, place, rows, *refs):
            n = PAIR[place]
            v = part[n, rows, :].astype(F32)
            for ref in refs:
                v = v + ref[rows, :].astype(F32)
            part[n, rows, :] = v.astype(BF16)

        def joined(self, group):
            self.cross[group].wait_recv()
            self.join(*group, pl.ds(0, unit_rows))

        def leave(self, q):
            self.a[q].start()
            for copy in self.b[q]:
                copy.start()

        def early_side(self, q):
            (self.dm if q < 2 else self.dp)[q].start()

        def pass_two(self, q):
            self.a[q].wait_recv()
            self.add((2, 0), quarter(q), rya.at[self.phase])
            self.c[q].start()

        def pass_y(self, h):
            for q in (2 * h, 2 * h + 1):
                for copy in self.b[q]:
                    copy.wait_recv()
            self.add((0, 1), halves(h), rzb.at[self.phase, 0], rzb.at[self.phase, 1])
            self.e[h].start()

        def finish(self, idle):
            p = self.phase
            for q in QUARTERS:
                self.c[q].wait_recv()
                side, out = ((1, 0), self.dp) if q < 2 else ((-1, 0), self.dm)
                self.add(side, quarter(q), rzc.at[p])
                out[q].start()
            idle()
            for copy in (*self.e, *self.dp, *self.dm):
                copy.wait_recv()
            return (
                part[0].astype(F32) + rzd[p, 0].astype(F32) + rzd[p, 1].astype(F32) + rye[p].astype(F32)
            )

    def units(buf, group):
        a, b = group
        m = 2 * (b - a) * unit_rows
        return jnp.concatenate([buf[a:b], buf[PAIRS + a : PAIRS + b]], axis=0).reshape(m, width)

    def hidden_rows(group):
        return pl.ds(2 * group[0] * unit_rows, 2 * (group[1] - group[0]) * unit_rows)

    def put_parts(group, v):
        a, b = group
        v = v.astype(BF16).reshape(2, b - a, unit_rows, width)
        part[a:b] = v[0]
        part[PAIRS + a : PAIRS + b] = v[1]

    lanes = [pl.ds(0, 512), pl.ds(512, w1.shape[0] - 512)]
    all_lanes = pl.ds(0, w1.shape[0])

    def up(group, lanes):
        pre1[hidden_rows(group), lanes] = dot_t(units(g1, group), w1[lanes, :])

    def activate(group):
        r = hidden_rows(group)

        def act(i, _):
            s = pl.ds(pl.multiple_of(r.start + i * 32, 32), 32)
            hid[s, :] = gelu(pre1[s, :]).astype(BF16)
            return 0

        lax.fori_loop(0, r.size // 32, act, 0)

    def down(group):
        put_parts(group, dot(hid[hidden_rows(group), :], w2[...]))

    def up_back(group, lanes):
        r = hidden_rows(group)
        hid[r, lanes] = (dot_t(units(g3, group), w2[lanes, :]) * pre1[r, lanes]).astype(BF16)

    def down_back(group):
        put_parts(group, dot(hid[hidden_rows(group), :], w1[...]))

    def scatter_mlp(phase, compute, aside, idle):
        s = Scatter(phase)
        compute(FAR)
        s.cross[5, 7].start()
        s.cross[7, 8].start()
        aside()
        s.joined((5, 7))
        for q in QUARTERS:
            for copy in s.b[q]:
                copy.start()
        s.joined((7, 8))
        for q in QUARTERS:
            s.a[q].start()
        compute(NEAR)
        for group in ((4, 5), (1, 4), (0, 1)):
            s.cross[group].start()
        s.joined((4, 5))
        s.pass_two(0)
        s.pass_two(3)
        s.joined((1, 4))
        s.early_side(0)
        s.pass_two(1)
        s.early_side(3)
        s.pass_y(0)
        s.pass_two(2)
        s.early_side(1)
        s.early_side(2)
        s.joined((0, 1))
        s.pass_y(1)
        return s.finish(idle)

    near_row = iota((unit_rows, unit_rows), 0)
    far_row = iota((unit_rows, unit_rows), 1)

    def spread(a, b):
        return one_hot(far_row == lax.rem(near_row, a) * b + near_row // a)

    blocks = width // 128
    vgain[...] = line(vgain_ref, 0, blocks)
    v = dot(spread(merged_own, 4), x_ref[...])
    cen = v - jnp.mean(v, -1, keepdims=True)
    inv = lax.rsqrt(jnp.mean(cen * cen, -1, keepdims=True) + VIS_EPS)
    hat = cen * inv
    xhat[...] = hat
    xinv[...] = inv
    g1[0] = (hat * vgain[...]).astype(BF16)
    own[...] = v

    row = iota((1, dest_ref.size), 1)
    dest = line(dest_ref, 0, dest_ref.shape[0])
    dest_seq = jnp.zeros_like(dest)
    for n in range(1, 8):
        dest_seq += jnp.where(dest >= n * seq_len, 1, 0)
    inside = row & 31
    row_grp = row >> 7
    row_z = (row >> 5) & 3
    row_y = (row >> 4) & 1
    row_core = (row >> 3) & 1
    key = jnp.where(
        dest_seq == grp, ((row_grp & 6) | ((row_grp & 1) ^ row_y ^ yhi)) * 32 + inside, -1
    )
    token = (dest - dest_seq * seq_len + 1).astype(F32)
    tok = jnp.sum(jnp.where(key == iota((slots, row.shape[1]), 0), token, 0.0), -1, keepdims=True) - 1.0
    tcol[...] = tok.astype(jnp.int32)
    trow[...] = turned(tok).astype(jnp.int32)
    step_z = (row_z - z) & 3
    step_y = row_y ^ yhi
    pair = jnp.where(
        step_y == 0,
        jnp.where(step_z == 0, 0, jnp.where(step_z == 1, 1, jnp.where(step_z == 3, 2, 4))),
        jnp.where(step_z == 0, 3, jnp.where(step_z == 1, 5, jnp.where(step_z == 3, 6, 7))),
    )
    mine = ((row_grp >> 1) == x) & (((row_grp & 1) ^ row_y) == (ylo ^ yhi))
    key = jnp.where(mine, ((row_core ^ core) * PAIRS + pair) * merged_own + (row & 7), -1)
    slot = (dest_seq * 32 + inside).astype(F32)
    slot = jnp.sum(jnp.where(key == iota((merged_all, row.shape[1]), 0), slot, 0.0), -1, keepdims=True)
    scol[...] = slot.astype(jnp.int32)
    srow[...] = turned(slot).astype(jnp.int32)
    pl.semaphore_wait(barrier, 11)

    def exchange(src, dst, n):
        copies = []
        for k in range(1, 8):
            g, where = peer(k)
            copies.append(pltpu.make_async_remote_copy(
                src_ref=src.at[g], dst_ref=dst.at[grp],
                send_sem=esend.at[n, k - 1], recv_sem=erecv.at[n, k - 1],
                device_id=where, device_id_type=MESH,
            ))
        copies.append(pltpu.make_async_copy(src.at[grp], dst.at[grp], lsem.at[5 + n]))
        for copy in copies:
            copy.start()
        return copies

    def exchange_wait(copies):
        for copy in copies:
            copy.wait()

    holder = {}

    def pick():
        cot_load.wait()
        v = dot(one_hot(iota((slots, seq_len), 1) == tcol[...]), cot[...])
        picked[...] = v.astype(BF16).reshape(picked.shape)
        holder["cot"] = exchange(picked, returned, 0)

    def up_near(h):
        if h == 0:
            w1_load.wait()
        up(NEAR, lanes[h])
        if h == 1:
            activate(NEAR)
            ls[...] = line(ls_ref, 0, blocks)
            for q in range(4):
                pgain[quarter(q), :] = jnp.broadcast_to(line(pgain_ref, q * blocks, blocks), (merged_own, width))

    def up_far():
        up(FAR, all_lanes)
        activate(FAR)

    def slopes():
        def act(i, _):
            r = pl.ds(pl.multiple_of(i * 32, 32), 32)
            pre1[r, :] = gelu_slope(pre1[r, :])
            return 0

        lax.fori_loop(0, UNITS, act, 0)

    gather(0, g1, up_near, up_far)
    w2_load.wait()
    total = scatter_mlp(0, down, pick, slopes)

    def over_merged(v):
        s = jnp.sum(v, -1, keepdims=True).reshape(4, merged_own, 1).sum(axis=0) * (1.0 / (4 * width))
        return jnp.concatenate([s] * 4, axis=0)

    y = (own[...] + ls[...] * total).astype(BF16).astype(F32)
    cen = y - over_merged(y)
    inv = lax.rsqrt(over_merged(cen * cen) + PROJ_EPS)
    hat = cen * inv
    mhat[...] = hat
    minv[...] = inv
    g2[0] = (hat * pgain[...]).astype(BF16)

    def ready(h):
        if h == 0:
            wp_load.wait()
            exchange_wait(holder["cot"])
            back[...] = dot(one_hot(iota((merged_all, slots), 1) == scol[...]), returned[...].reshape(slots, -1))

    def project():
        free_part()
        for q in range(4):
            lhs = g2[:, quarter(q), :].reshape(merged_all, width)
            v = dot(lhs, wp[pl.ds(q * width, width), :])
            if q == 0:
                pre2[...] = v
            else:
                pre2[...] += v
        hid2[...] = (back[...] * gelu_slope(pre2[...])).astype(BF16)

    def project_back(q):
        v = dot_t(hid2[...], wp[pl.ds(q * width, width), :])
        part[:, quarter(q), :] = v.astype(BF16).reshape(UNITS, merged_own, width)

    def send_projected():
        v = dot(one_hot(iota((slots, merged_all), 0) == srow[...]), gelu(pre2[...]).astype(BF16))
        out_slots[...] = v.astype(BF16).reshape(out_slots.shape)
        holder["proj"] = exchange(out_slots, arrived, 1)

    gather(1, g2, ready, project)
    s = Scatter(1)

    def joined(q):
        s.cross[q].wait_recv()
        s.join(0, PAIRS, quarter(q))
        s.leave(q)
        s.early_side(q)

    for n, q in enumerate(QUARTERS):
        project_back(q)
        s.cross[q].start()
        if n:
            joined(QUARTERS[n - 1])
    s.pass_two(0)
    joined(QUARTERS[3])
    for q in QUARTERS[1:]:
        s.pass_two(q)
        if q != 3:
            s.pass_y(q - 1)
    total = s.finish(send_projected)
    hat = mhat[...]
    v = total * pgain[...]
    dm = minv[...] * (v - over_merged(v) - hat * over_merged(v * hat))
    dy = dm.astype(BF16).astype(F32)
    own[...] = dy
    g3[0] = (dy * ls[...]).astype(BF16)

    def fill():
        text_load.wait()
        exchange_wait(holder["proj"])
        block = 128
        flat = arrived[...].reshape(slots, -1)

        def step(i, _):
            r0 = pl.multiple_of(i * block, block)
            r = pl.ds(r0, block)
            hot = jnp.where(iota((block, slots), 0) + r0 == trow[...], 1.0, 0.0)
            v = dot(hot.astype(BF16), flat)
            filled = jnp.sum(hot, -1, keepdims=True) > 0.5
            seq[r, :] = jnp.where(filled, v, seq[r, :].astype(F32)).astype(BF16)
            return 0

        lax.fori_loop(0, seq_len // block, step, 0)
        holder["seq"] = pltpu.make_async_copy(seq, seq_hbm, lsem.at[7])
        holder["seq"].start()

    gather(2, g3, lambda h: up_back(NEAR, lanes[h]), lambda: up_back(FAR, all_lanes))
    free_part()
    total = scatter_mlp(2, down_back, lambda: None, fill)
    hat = xhat[...]
    v = total * vgain[...]
    g = own[...] + xinv[...] * (
        v - jnp.mean(v, -1, keepdims=True) - hat * jnp.mean(v * hat, -1, keepdims=True)
    )
    grad_ref[...] = dot(spread(4, merged_own), g.astype(BF16)).astype(BF16)
    free_part()
    holder["seq"].wait()


def junction(x, vgain, ls, pgain, dest, w1, w2, wp, text, cot):
    unit_rows, width = x.shape
    hidden = w1.shape[0]
    cols = wp.shape[1]
    all_rows = UNITS * unit_rows
    merged_all = all_rows // 4
    vmem = pl.BlockSpec(memory_space=pltpu.VMEM)
    hbm = pl.BlockSpec(memory_space=pl.ANY)
    V = pltpu.VMEM
    unit = (unit_rows, width)
    scratch = [
        V(w1.shape, BF16), V(w2.shape, BF16), V(wp.shape, BF16), V(cot.shape, BF16), V(text.shape, BF16),
        *[V((UNITS, *unit), BF16)] * 4,
        V((3, PAIRS, *unit), BF16),
        V((3, *unit), BF16), V((3, *unit), BF16), V((3, 2, *unit), BF16), V((3, *unit), BF16), V((3, 2, *unit), BF16),
        V((all_rows, hidden), F32), V((all_rows, hidden), BF16), V((merged_all, cols), F32), V((merged_all, cols), BF16),
        V((merged_all, cols), F32),
        *[V((8, 32, cols), BF16)] * 4,
        V(unit, F32), V((unit_rows, 1), F32), V(unit, F32), V(unit, F32), V((unit_rows, 1), F32),
        V((1, width), F32), V((1, width), F32), V(unit, F32),
        V((merged_all, 1), jnp.int32), V((1, merged_all), jnp.int32), V((256, 1), jnp.int32), V((1, 256), jnp.int32),
        pltpu.SemaphoreType.DMA((3 * PHASE_MSGS,)), pltpu.SemaphoreType.DMA((3 * PHASE_MSGS,)),
        pltpu.SemaphoreType.DMA((2, 7)), pltpu.SemaphoreType.DMA((2, 7)),
        pltpu.SemaphoreType.DMA((8,)),
    ]
    return pl.pallas_call(
        kernel,
        out_shape=(jax.ShapeDtypeStruct(text.shape, BF16), jax.ShapeDtypeStruct(x.shape, BF16)),
        in_specs=[vmem] * 5 + [hbm] * 5,
        out_specs=(hbm, vmem),
        scratch_shapes=scratch,
        name="junction",
        compiler_params=pltpu.CompilerParams(
            collective_id=0, has_side_effects=True, vmem_limit_bytes=67_000_000
        ),
    )(x, vgain, ls, pgain, dest, w1, w2, wp, text, cot)


def leave_kernel(seq_in, grad_in, seq_out, grad_out, seq, grad, sem_in, sem_out):
    parts = sem_in.shape[0] - 1
    rows = seq.shape[0] // parts
    moves = [(grad_in, grad, grad_out)]
    for n in range(parts):
        r = pl.ds(n * rows, rows)
        moves.append((seq_in.at[r], seq.at[r], seq_out.at[r]))
    take = [pltpu.make_async_copy(src, mid, sem_in.at[n]) for n, (src, mid, _) in enumerate(moves)]
    give = [pltpu.make_async_copy(mid, dst, sem_out.at[n]) for n, (_, mid, dst) in enumerate(moves)]
    for copy in take:
        copy.start()
    for first, second in zip(take, give):
        first.wait()
        second.start()
    for copy in give:
        copy.wait()


def leave(seq, grad):
    hbm = pl.BlockSpec(memory_space=pl.ANY)
    parts = 6
    return pl.pallas_call(
        leave_kernel,
        out_shape=(jax.ShapeDtypeStruct(seq.shape, BF16), jax.ShapeDtypeStruct(grad.shape, BF16)),
        in_specs=[hbm, hbm],
        out_specs=(hbm, hbm),
        scratch_shapes=[
            pltpu.VMEM(seq.shape, BF16), pltpu.VMEM(grad.shape, BF16),
            pltpu.SemaphoreType.DMA((parts + 1,)), pltpu.SemaphoreType.DMA((parts + 1,)),
        ],
        name="leave",
    )(seq, grad)


def per_device(
    vision_in, vis_gain, first_weight, second_weight, layer_scale,
    proj_gain, proj_weight, text_embed, dest_row, cotangent,
):
    return leave(*junction(
        vision_in, vis_gain.reshape(-1, 128), layer_scale.reshape(-1, 128), proj_gain.reshape(-1, 128),
        dest_row.reshape(-1, 128), first_weight.T, second_weight, proj_weight, text_embed, cotangent,
    ))


def solution(mesh):
    torus = Mesh(mesh.devices.reshape(4, 2, 4, 2, 2), AXES)
    in_specs = (
        P((*GRP, *TP), None), P(), P(None, TP), P(TP, None), P(), P(), P(None, TP),
        P(GRP, TP), P(), P(GRP, TP),
    )
    out_specs = (P(GRP, TP), P((*GRP, *TP), None))
    return jax.shard_map(per_device, mesh=torus, in_specs=in_specs, out_specs=out_specs, check_vma=False)
```

```python
import functools

import jax
import jax.numpy as jnp
from jax import lax
from jax.experimental import pallas as pl
from jax.experimental.pallas import tpu as pltpu
from jax.sharding import Mesh
from jax.sharding import PartitionSpec as P

AXES = ("x", "ylo", "z", "yhi", "core")
GRP = ("x", "ylo")
TP = ("z", "yhi", "core")
MESH = pl.DeviceIdType.MESH
VIS_EPS = 1e-06
PROJ_EPS = 1e-05
F32 = jnp.float32
BF16 = jnp.bfloat16

PLACES = [(0, 0), (1, 0), (-1, 0), (0, 1), (2, 0), (1, 1), (-1, 1), (2, 1)]
PAIR = {place: n for n, place in enumerate(PLACES)}
PAIRS = 8
UNITS = 16
NEAR = (0, 5)
FAR = (5, 8)
QUARTERS = (0, 3, 1, 2)
AG_MSGS = 30
RS_MSGS = 32
PHASE_MSGS = AG_MSGS + RS_MSGS


def erf_half(u):
    return 0.5 * (1.0 + lax.erf(u * 0.7071067811865476))


def gelu(u):
    return u * erf_half(u)


def gelu_slope(u):
    return erf_half(u) + u * (jnp.exp(-0.5 * u * u) * 0.3989422804014327)


def dot(a, b):
    return jnp.dot(a, b, preferred_element_type=F32)


def dot_t(a, b):
    return lax.dot_general(a, b, (((1,), (1,)), ((), ())), preferred_element_type=F32)


def iota(shape, dim):
    return lax.broadcasted_iota(jnp.int32, shape, dim)


def one_hot(cond):
    return jnp.where(cond, 1.0, 0.0).astype(BF16)


def line(ref, start, count):
    return jnp.concatenate([ref[pl.ds(start + n, 1), :] for n in range(count)], axis=1)


def turned(col):
    n = col.shape[0]
    return jnp.sum(jnp.where(iota((n, n), 0) == iota((n, n), 1), col, 0.0), 0, keepdims=True)


def kernel(
    x_ref, vgain_ref, ls_ref, pgain_ref, dest_ref,
    w1_hbm, w2_hbm, wp_hbm, text_hbm, cot_hbm,
    seq_hbm, grad_ref,
    w1, w2, wp, cot, seq,
    g1, g2, g3, part, rcore, rya, rye, rzb, rzc, rzd,
    pre1, hid, pre2, hid2, back, half_sum,
    out_slots, arrived, picked, returned,
    xhat, xinv, own, mhat, minv, vgain, ls, pgain,
    scol, srow, tcol, trow,
    ssem, rsem, esend, erecv, lsem,
):
    x = lax.axis_index("x")
    ylo = lax.axis_index("ylo")
    z = lax.axis_index("z")
    yhi = lax.axis_index("yhi")
    core = lax.axis_index("core")
    grp = 2 * x + ylo
    unit_rows, width = x_ref.shape
    half = unit_rows // 2
    merged_own = unit_rows // 4
    merged_all = UNITS * merged_own
    slots = 8 * 32
    seq_len = cot.shape[0]
    to = {
        "y": {"ylo": 1 - ylo, "yhi": 1 - yhi},
        "z+": {"z": lax.rem(z + 1, 4)},
        "z-": {"z": lax.rem(z + 3, 4)},
        "c": {"core": 1 - core},
    }

    def peer(k):
        g = lax.rem(grp + k, 8)
        return g, {"x": g // 2, "ylo": lax.rem(g, 2)}

    barrier = pltpu.get_barrier_semaphore()
    for d in to.values():
        pl.semaphore_signal(barrier, inc=1, device_id=d, device_id_type=MESH)
    for k in range(1, 8):
        pl.semaphore_signal(barrier, inc=1, device_id=peer(k)[1], device_id_type=MESH)

    loads = []
    for n, (src, dst) in enumerate(((cot_hbm, cot), (w1_hbm, w1), (w2_hbm, w2), (wp_hbm, wp), (text_hbm, seq))):
        copy = pltpu.make_async_copy(src, dst, lsem.at[n])
        copy.start()
        loads.append(copy)
    cot_load, w1_load, w2_load, wp_load, text_load = loads

    sent = []

    def remote(src, dst, where, n):
        copy = pltpu.make_async_remote_copy(
            src_ref=src, dst_ref=dst, send_sem=ssem.at[n], recv_sem=rsem.at[n],
            device_id=to[where], device_id_type=MESH,
        )
        sent.append(copy)
        return copy

    def free_part():
        for copy in sent:
            copy.wait_send()
        sent.clear()

    def halves(h):
        return pl.ds(h * half, half)

    def quarter(q):
        return pl.ds(q * merged_own, merged_own)

    edges = [width // 512 * 128 * n + (128 if n else 0) for n in range(4)] + [width]

    def col_quarter(q):
        return pl.ds(edges[q], edges[q + 1] - edges[q])

    def col_half(h):
        return pl.ds(edges[2 * h], edges[2 * h + 2] - edges[2 * h])

    def gather(phase, buf, middle, tail, late):
        count = iter(range(phase * PHASE_MSGS, phase * PHASE_MSGS + AG_MSGS))

        def msg(src, dst, where, cols=None):
            s, d = buf.at[PAIR[src]], buf.at[PAIR[dst]]
            if cols is not None:
                s, d = s.at[:, cols], d.at[:, cols]
            return remote(s, d, where, next(count))

        def cross(first, last, cols=pl.ds(0, width)):
            return remote(
                buf.at[first:last, :, cols], buf.at[PAIRS + first : PAIRS + last, :, cols], "c", next(count)
            )

        own_zp = [msg((0, 0), (-1, 0), "z+", col_quarter(q)) for q in range(4)]
        own_zm = [msg((0, 0), (1, 0), "z-", col_quarter(q)) for q in range(4)]
        own_y = [msg((0, 0), (0, 1), "y", col_half(h)) for h in range(2)]
        two = {q: msg((-1, 0), (2, 0), "z+", col_quarter(q)) for q in (0, 1)}
        two |= {q: msg((1, 0), (2, 0), "z-", col_quarter(q)) for q in (3, 2)}
        y_zp = [msg((0, 1), (-1, 1), "z+", col_half(h)) for h in range(2)]
        y_zm = [msg((0, 1), (1, 1), "z-", col_half(h)) for h in range(2)]
        two_y = [msg((2, 0), (2, 1), "y", col_quarter(q)) for q in range(4)]
        c_own, c_side, c_y, c_two = (cross(*r) for r in ((0, 1), (1, 3), (3, 4), (4, 5)))
        c_far = [cross(5, 7, col_half(h)) for h in range(2)]
        c_last = [cross(7, 8, col_half(h)) for h in range(2)]
        for copy in (
            own_zp[0], own_zm[3], own_y[0], own_zp[1], own_zm[2], own_y[1], own_zp[2], own_zm[1], c_own,
        ):
            copy.start()
        for p, m in ((0, 3), (1, 2)):
            own_zp[p].wait_recv()
            two[p].start()
            own_zm[m].wait_recv()
            two[m].start()
        own_zp[3].start()
        own_zm[0].start()
        own_y[0].wait_recv()
        y_zp[0].start()
        y_zm[0].start()
        two[0].wait_recv()
        two_y[0].start()
        own_y[1].wait_recv()
        y_zp[1].start()
        y_zm[1].start()
        c_y.start()
        for q in (1, 3, 2):
            two[q].wait_recv()
            two_y[q].start()
        c_two.start()
        for copy in (own_zp[2], own_zp[3], own_zm[1], own_zm[0]):
            copy.wait_recv()
        c_side.start()
        for copy in (c_own, c_y, c_two, c_side):
            copy.wait_recv()
        for h in range(2):
            middle(h)
            y_zp[h].wait_recv()
            y_zm[h].wait_recv()
            c_far[h].start()
            for q in (2 * h, 2 * h + 1):
                two_y[q].wait_recv()
            c_last[h].start()
        for h, step in ((0, tail), (1, late)):
            c_far[h].wait_recv()
            c_last[h].wait_recv()
            step()

    class Scatter:
        def __init__(self, phase):
            count = iter(range(phase * PHASE_MSGS + AG_MSGS, (phase + 1) * PHASE_MSGS))
            self.phase = phase

            def msg(place, rows, dst, where):
                return remote(part.at[PAIR[place], rows], dst.at[rows], where, next(count))

            def cross(first, last, rows):
                return remote(
                    part.at[PAIRS + first : PAIRS + last, rows], rcore.at[phase, first:last, rows], "c", next(count)
                )

            if phase == 1:
                self.cross = [cross(0, PAIRS, quarter(q)) for q in range(4)]
            else:
                everything = pl.ds(0, unit_rows)
                self.cross = {g: cross(*g, everything) for g in ((5, 7), (7, 8), (4, 5), (1, 4), (0, 1))}
            self.a = [msg((2, 1), quarter(q), rya.at[phase], "y") for q in range(4)]
            self.b = [
                (msg((1, 1), quarter(q), rzb.at[phase, 0], "z+"), msg((-1, 1), quarter(q), rzb.at[phase, 1], "z-"))
                for q in range(4)
            ]
            self.c = [msg((2, 0), quarter(q), rzc.at[phase], "z+" if q < 2 else "z-") for q in range(4)]
            self.dp = [msg((1, 0), quarter(q), rzd.at[phase, 0], "z+") for q in range(4)]
            self.dm = [msg((-1, 0), quarter(q), rzd.at[phase, 1], "z-") for q in range(4)]
            self.e = [msg((0, 1), halves(h), rye.at[phase], "y") for h in range(2)]

        def join(self, first, last, rows):
            for n in range(first, last):
                v = part[n, rows, :].astype(F32) + rcore[self.phase, n, rows, :].astype(F32)
                part[n, rows, :] = v.astype(BF16)

        def add(self, place, rows, *refs):
            n = PAIR[place]
            v = part[n, rows, :].astype(F32)
            for ref in refs:
                v = v + ref[rows, :].astype(F32)
            part[n, rows, :] = v.astype(BF16)

        def joined(self, group):
            self.cross[group].wait_recv()
            self.join(*group, pl.ds(0, unit_rows))

        def leave(self, q):
            self.a[q].start()
            for copy in self.b[q]:
                copy.start()

        def early_side(self, q):
            (self.dm if q < 2 else self.dp)[q].start()

        def pass_two(self, q):
            self.a[q].wait_recv()
            self.add((2, 0), quarter(q), rya.at[self.phase])
            self.c[q].start()

        def pass_y(self, h):
            for q in (2 * h, 2 * h + 1):
                for copy in self.b[q]:
                    copy.wait_recv()
            self.add((0, 1), halves(h), rzb.at[self.phase, 0], rzb.at[self.phase, 1])
            self.e[h].start()

        def finish(self, idle):
            p = self.phase
            for q in QUARTERS:
                self.c[q].wait_recv()
                side, out = ((1, 0), self.dp) if q < 2 else ((-1, 0), self.dm)
                self.add(side, quarter(q), rzc.at[p])
                out[q].start()
            idle()
            for copy in (*self.e, *self.dp, *self.dm):
                copy.wait_recv()
            return (
                part[0].astype(F32) + rzd[p, 0].astype(F32) + rzd[p, 1].astype(F32) + rye[p].astype(F32)
            )

    def units(buf, group, cols=pl.ds(0, width)):
        a, b = group
        m = 2 * (b - a) * unit_rows
        both = jnp.concatenate([buf[a:b, :, cols], buf[PAIRS + a : PAIRS + b, :, cols]], axis=0)
        return both.reshape(m, cols.size)

    def hidden_rows(group):
        return pl.ds(2 * group[0] * unit_rows, 2 * (group[1] - group[0]) * unit_rows)

    def put_parts(group, v):
        a, b = group
        v = v.astype(BF16).reshape(2, b - a, unit_rows, width)
        part[a:b] = v[0]
        part[PAIRS + a : PAIRS + b] = v[1]

    lanes = [[pl.ds(512, w1.shape[0] - 512)], [pl.ds(256, 256), pl.ds(0, 256)]]

    def far_first(buf, weights, h):
        return dot_t(units(buf, FAR, col_half(h)), weights[:, col_half(h)])

    def up(group, lanes):
        pre1[hidden_rows(group), lanes] = dot_t(units(g1, group), w1[lanes, :])

    def activate(group):
        r = hidden_rows(group)

        def act(i, _):
            s = pl.ds(pl.multiple_of(r.start + i * 32, 32), 32)
            hid[s, :] = gelu(pre1[s, :]).astype(BF16)
            return 0

        lax.fori_loop(0, r.size // 32, act, 0)

    def down(group):
        put_parts(group, dot(hid[hidden_rows(group), :], w2[...]))

    def up_back(group, lanes):
        r = hidden_rows(group)
        hid[r, lanes] = (dot_t(units(g3, group), w2[lanes, :]) * pre1[r, lanes]).astype(BF16)

    def up_back_far(h):
        r = hidden_rows(FAR)
        if h == 0:
            half_sum[...] = far_first(g3, w2, 0)
        else:
            hid[r, :] = ((half_sum[...] + far_first(g3, w2, 1)) * pre1[r, :]).astype(BF16)

    def down_back(group):
        put_parts(group, dot(hid[hidden_rows(group), :], w1[...]))

    def scatter_mlp(phase, compute, aside, idle):
        s = Scatter(phase)
        compute(FAR)
        s.cross[5, 7].start()
        s.cross[7, 8].start()
        aside()
        s.joined((5, 7))
        for q in QUARTERS:
            for copy in s.b[q]:
                copy.start()
        s.joined((7, 8))
        for q in QUARTERS:
            s.a[q].start()
        compute(NEAR)
        for group in ((4, 5), (1, 4), (0, 1)):
            s.cross[group].start()
        s.joined((4, 5))
        s.pass_two(0)
        s.pass_two(3)
        s.joined((1, 4))
        s.early_side(0)
        s.pass_two(1)
        s.early_side(3)
        s.pass_y(0)
        s.pass_two(2)
        s.early_side(1)
        s.early_side(2)
        s.joined((0, 1))
        s.pass_y(1)
        return s.finish(idle)

    near_row = iota((unit_rows, unit_rows), 0)
    far_row = iota((unit_rows, unit_rows), 1)

    def spread(a, b):
        return one_hot(far_row == lax.rem(near_row, a) * b + near_row // a)

    blocks = width // 128
    vgain[...] = line(vgain_ref, 0, blocks)
    v = dot(spread(merged_own, 4), x_ref[...])
    cen = v - jnp.mean(v, -1, keepdims=True)
    inv = lax.rsqrt(jnp.mean(cen * cen, -1, keepdims=True) + VIS_EPS)
    hat = cen * inv
    xhat[...] = hat
    xinv[...] = inv
    g1[0] = (hat * vgain[...]).astype(BF16)
    own[...] = v

    row = iota((1, dest_ref.size), 1)
    dest = line(dest_ref, 0, dest_ref.shape[0])
    dest_seq = jnp.zeros_like(dest)
    for n in range(1, 8):
        dest_seq += jnp.where(dest >= n * seq_len, 1, 0)
    inside = row & 31
    row_grp = row >> 7
    row_z = (row >> 5) & 3
    row_y = (row >> 4) & 1
    row_core = (row >> 3) & 1
    key = jnp.where(
        dest_seq == grp, ((row_grp & 6) | ((row_grp & 1) ^ row_y ^ yhi)) * 32 + inside, -1
    )
    token = (dest - dest_seq * seq_len + 1).astype(F32)
    tok = jnp.sum(jnp.where(key == iota((slots, row.shape[1]), 0), token, 0.0), -1, keepdims=True) - 1.0
    tcol[...] = tok.astype(jnp.int32)
    trow[...] = turned(tok).astype(jnp.int32)
    step_z = (row_z - z) & 3
    step_y = row_y ^ yhi
    pair = jnp.where(
        step_y == 0,
        jnp.where(step_z == 0, 0, jnp.where(step_z == 1, 1, jnp.where(step_z == 3, 2, 4))),
        jnp.where(step_z == 0, 3, jnp.where(step_z == 1, 5, jnp.where(step_z == 3, 6, 7))),
    )
    mine = ((row_grp >> 1) == x) & (((row_grp & 1) ^ row_y) == (ylo ^ yhi))
    key = jnp.where(mine, ((row_core ^ core) * PAIRS + pair) * merged_own + (row & 7), -1)
    slot = (dest_seq * 32 + inside).astype(F32)
    slot = jnp.sum(jnp.where(key == iota((merged_all, row.shape[1]), 0), slot, 0.0), -1, keepdims=True)
    scol[...] = slot.astype(jnp.int32)
    srow[...] = turned(slot).astype(jnp.int32)
    pl.semaphore_wait(barrier, 11)

    def exchange(src, dst, n):
        copies = []
        for k in range(1, 8):
            g, where = peer(k)
            copies.append(pltpu.make_async_remote_copy(
                src_ref=src.at[g], dst_ref=dst.at[grp],
                send_sem=esend.at[n, k - 1], recv_sem=erecv.at[n, k - 1],
                device_id=where, device_id_type=MESH,
            ))
        copies.append(pltpu.make_async_copy(src.at[grp], dst.at[grp], lsem.at[5 + n]))
        for copy in copies:
            copy.start()
        return copies

    def exchange_wait(copies):
        for copy in copies:
            copy.wait()

    holder = {}

    def pick():
        cot_load.wait()
        v = dot(one_hot(iota((slots, seq_len), 1) == tcol[...]), cot[...])
        picked[...] = v.astype(BF16).reshape(picked.shape)
        holder["cot"] = exchange(picked, returned, 0)

    def up_near(h):
        if h == 0:
            w1_load.wait()
        for n in lanes[h]:
            up(NEAR, n)

    def up_far(h):
        r = hidden_rows(FAR)
        if h == 0:
            pre1[r, :] = far_first(g1, w1, 0)
        else:
            pre1[r, :] += far_first(g1, w1, 1)
            activate(FAR)

    def after_first():
        ls[...] = line(ls_ref, 0, blocks)
        for q in range(4):
            pgain[quarter(q), :] = jnp.broadcast_to(line(pgain_ref, q * blocks, blocks), (merged_own, width))
        pick()
        slopes()

    def slopes():
        def act(i, _):
            r = pl.ds(pl.multiple_of(i * 32, 32), 32)
            pre1[r, :] = gelu_slope(pre1[r, :])
            return 0

        lax.fori_loop(0, UNITS, act, 0)

    gather(0, g1, up_near, lambda: up_far(0), lambda: up_far(1))
    w2_load.wait()
    total = scatter_mlp(0, down, lambda: activate(NEAR), after_first)

    def over_merged(v):
        s = jnp.sum(v, -1, keepdims=True).reshape(4, merged_own, 1).sum(axis=0) * (1.0 / (4 * width))
        return jnp.concatenate([s] * 4, axis=0)

    y = (own[...] + ls[...] * total).astype(BF16).astype(F32)
    cen = y - over_merged(y)
    inv = lax.rsqrt(over_merged(cen * cen) + PROJ_EPS)
    hat = cen * inv
    mhat[...] = hat
    minv[...] = inv
    g2[0] = (hat * pgain[...]).astype(BF16)

    def ready(h):
        if h == 0:
            wp_load.wait()
            exchange_wait(holder["cot"])
            back[...] = dot(one_hot(iota((merged_all, slots), 1) == scol[...]), returned[...].reshape(slots, -1))

    def project(h):
        for q in range(4):
            cols = col_half(h)
            lhs = g2[:, quarter(q), cols].reshape(merged_all, cols.size)
            v = dot(lhs, wp[pl.ds(q * width + cols.start, cols.size), :])
            if q == h == 0:
                pre2[...] = v
            else:
                pre2[...] += v
        if h == 1:
            hid2[...] = (back[...] * gelu_slope(pre2[...])).astype(BF16)
            free_part()

    def project_back(q):
        v = dot_t(hid2[...], wp[pl.ds(q * width, width), :])
        part[:, quarter(q), :] = v.astype(BF16).reshape(UNITS, merged_own, width)

    def send_projected():
        v = dot(one_hot(iota((slots, merged_all), 0) == srow[...]), gelu(pre2[...]).astype(BF16))
        out_slots[...] = v.astype(BF16).reshape(out_slots.shape)
        holder["proj"] = exchange(out_slots, arrived, 1)

    gather(1, g2, ready, lambda: project(0), lambda: project(1))
    s = Scatter(1)

    def joined(q):
        s.cross[q].wait_recv()
        s.join(0, PAIRS, quarter(q))
        s.leave(q)
        s.early_side(q)

    for n, q in enumerate(QUARTERS):
        project_back(q)
        s.cross[q].start()
        if n:
            joined(QUARTERS[n - 1])
    s.pass_two(0)
    joined(QUARTERS[3])
    for q in QUARTERS[1:]:
        s.pass_two(q)
        if q != 3:
            s.pass_y(q - 1)
    total = s.finish(send_projected)
    hat = mhat[...]
    v = total * pgain[...]
    dm = minv[...] * (v - over_merged(v) - hat * over_merged(v * hat))
    dy = dm.astype(BF16).astype(F32)
    own[...] = dy
    g3[0] = (dy * ls[...]).astype(BF16)

    def fill():
        text_load.wait()
        exchange_wait(holder["proj"])
        block = 128
        flat = arrived[...].reshape(slots, -1)

        def step(i, _):
            r0 = pl.multiple_of(i * block, block)
            r = pl.ds(r0, block)
            hot = jnp.where(iota((block, slots), 0) + r0 == trow[...], 1.0, 0.0)
            v = dot(hot.astype(BF16), flat)
            filled = jnp.sum(hot, -1, keepdims=True) > 0.5
            seq[r, :] = jnp.where(filled, v, seq[r, :].astype(F32)).astype(BF16)
            return 0

        lax.fori_loop(0, seq_len // block, step, 0)
        holder["seq"] = pltpu.make_async_copy(seq, seq_hbm, lsem.at[7])
        holder["seq"].start()

    def back_near(h):
        for n in lanes[h]:
            up_back(NEAR, n)

    gather(2, g3, back_near, lambda: up_back_far(0), lambda: up_back_far(1))
    free_part()
    total = scatter_mlp(2, down_back, lambda: None, fill)
    hat = xhat[...]
    v = total * vgain[...]
    g = own[...] + xinv[...] * (
        v - jnp.mean(v, -1, keepdims=True) - hat * jnp.mean(v * hat, -1, keepdims=True)
    )
    grad_ref[...] = dot(spread(4, merged_own), g.astype(BF16)).astype(BF16)
    free_part()
    holder["seq"].wait()


def junction(x, vgain, ls, pgain, dest, w1, w2, wp, text, cot):
    unit_rows, width = x.shape
    hidden = w1.shape[0]
    cols = wp.shape[1]
    all_rows = UNITS * unit_rows
    merged_all = all_rows // 4
    vmem = pl.BlockSpec(memory_space=pltpu.VMEM)
    hbm = pl.BlockSpec(memory_space=pl.ANY)
    V = pltpu.VMEM
    unit = (unit_rows, width)
    scratch = [
        V(w1.shape, BF16), V(w2.shape, BF16), V(wp.shape, BF16), V(cot.shape, BF16), V(text.shape, BF16),
        *[V((UNITS, *unit), BF16)] * 4,
        V((3, PAIRS, *unit), BF16),
        V((3, *unit), BF16), V((3, *unit), BF16), V((3, 2, *unit), BF16), V((3, *unit), BF16), V((3, 2, *unit), BF16),
        V((all_rows, hidden), F32), V((all_rows, hidden), BF16), V((merged_all, cols), F32), V((merged_all, cols), BF16),
        V((merged_all, cols), F32), V((2 * (FAR[1] - FAR[0]) * unit_rows, hidden), F32),
        *[V((8, 32, cols), BF16)] * 4,
        V(unit, F32), V((unit_rows, 1), F32), V(unit, F32), V(unit, F32), V((unit_rows, 1), F32),
        V((1, width), F32), V((1, width), F32), V(unit, F32),
        V((merged_all, 1), jnp.int32), V((1, merged_all), jnp.int32), V((256, 1), jnp.int32), V((1, 256), jnp.int32),
        pltpu.SemaphoreType.DMA((3 * PHASE_MSGS,)), pltpu.SemaphoreType.DMA((3 * PHASE_MSGS,)),
        pltpu.SemaphoreType.DMA((2, 7)), pltpu.SemaphoreType.DMA((2, 7)),
        pltpu.SemaphoreType.DMA((8,)),
    ]
    return pl.pallas_call(
        kernel,
        out_shape=(jax.ShapeDtypeStruct(text.shape, BF16), jax.ShapeDtypeStruct(x.shape, BF16)),
        in_specs=[vmem] * 5 + [hbm] * 5,
        out_specs=(hbm, vmem),
        scratch_shapes=scratch,
        name="junction",
        compiler_params=pltpu.CompilerParams(
            collective_id=0, has_side_effects=True, vmem_limit_bytes=67_000_000
        ),
    )(x, vgain, ls, pgain, dest, w1, w2, wp, text, cot)


def leave_kernel(seq_in, grad_in, seq_out, grad_out, seq, grad, sem_in, sem_out):
    parts = sem_in.shape[0] - 1
    rows = seq.shape[0] // parts
    moves = [(grad_in, grad, grad_out)]
    for n in range(parts):
        r = pl.ds(n * rows, rows)
        moves.append((seq_in.at[r], seq.at[r], seq_out.at[r]))
    take = [pltpu.make_async_copy(src, mid, sem_in.at[n]) for n, (src, mid, _) in enumerate(moves)]
    give = [pltpu.make_async_copy(mid, dst, sem_out.at[n]) for n, (_, mid, dst) in enumerate(moves)]
    for copy in take:
        copy.start()
    for first, second in zip(take, give):
        first.wait()
        second.start()
    for copy in give:
        copy.wait()


def leave(seq, grad):
    hbm = pl.BlockSpec(memory_space=pl.ANY)
    parts = 6
    return pl.pallas_call(
        leave_kernel,
        out_shape=(jax.ShapeDtypeStruct(seq.shape, BF16), jax.ShapeDtypeStruct(grad.shape, BF16)),
        in_specs=[hbm, hbm],
        out_specs=(hbm, hbm),
        scratch_shapes=[
            pltpu.VMEM(seq.shape, BF16), pltpu.VMEM(grad.shape, BF16),
            pltpu.SemaphoreType.DMA((parts + 1,)), pltpu.SemaphoreType.DMA((parts + 1,)),
        ],
        name="leave",
    )(seq, grad)


def per_device(
    vision_in, vis_gain, first_weight, second_weight, layer_scale,
    proj_gain, proj_weight, text_embed, dest_row, cotangent,
):
    return leave(*junction(
        vision_in, vis_gain.reshape(-1, 128), layer_scale.reshape(-1, 128), proj_gain.reshape(-1, 128),
        dest_row.reshape(-1, 128), first_weight.T, second_weight, proj_weight, text_embed, cotangent,
    ))


def solution(mesh):
    torus = Mesh(mesh.devices.reshape(4, 2, 4, 2, 2), AXES)
    in_specs = (
        P((*GRP, *TP), None), P(), P(None, TP), P(TP, None), P(), P(), P(None, TP),
        P(GRP, TP), P(), P(GRP, TP),
    )
    out_specs = (P(GRP, TP), P((*GRP, *TP), None))
    return jax.shard_map(per_device, mesh=torus, in_specs=in_specs, out_specs=out_specs, check_vma=False)
```
